32 devices in a mesh: seq: 8 (over z, x), head: 4 (over y, core).
Axes of the slice: x: 2, y: 2, z: 4, core: 2. Of those that a mesh axis runs over, the one named last changes fastest.
Arguments:
- tokens: bfloat16 [4096, 4096], P('seq', 'head'), may hold values from -80 to 80, as said below
- w_query: bfloat16 [4096, 2048], P(None, 'head'), may hold values from -0.09375 to 0.09375
- w_key: bfloat16 [4096, 2048], P(None, 'head'), may hold values from -0.09375 to 0.09375
- w_value: bfloat16 [4096, 2048], P(None, 'head'), may hold values from -0.09375 to 0.09375
- w_out: bfloat16 [2048, 4096], P('head'), may hold values from -0.125 to 0.125
- block_bucket: int32 [32], P('seq'), may hold values from 0 to 47, as said below
Outputs:
- attended: bfloat16 [4096, 4096], P('seq', 'head')
The draws below stay inside these ranges and needn't reach their ends.
Inputs may be any that keep to these rules, and one draw needn't show every extreme that they name: `tokens`: hidden states of order one; a few rows may be far larger. `block_bucket`: no bucket holds more than 2 blocks, and some bucket holds exactly 2; an owner's buckets are numbered from its first id on and hold 2 blocks each except possibly its first and its last. The blocks of one index of seq belong to buckets of at most 1 block per owner, and some owner receives exactly 1 from every index of seq.
All inputs are finite; a program needn't handle non-finite values.
Results may differ from the reference program's by a relative error of at most 0.012.
The reference program's roundings to bfloat16 on the way (of `query`, `keys`, `values`, `weights` and `mixed`) count: a program that leaves them out, or rounds other values in their place, can miss the bound.
Values may be sent and summed in bfloat16 or wider, within the bound.
No kernel may reach another device: no remote copies, remote signals or barrier semaphores. Data moves between devices by JAX's collectives and lax.ppermute only.
A program may use at most 128 MiB of HBM per device.

```python
import jax
import jax.numpy as jnp
from jax import lax

D = 4096
HEADS = 16
HDIM = 128
BLOCK = 128
BMAX = 2
BLK_DEV = 4
NBLK = 32
TOKENS = 4096
BUCK_OWN = 6
N_SEQ = 8


def draw_tokens(key, part):
    first = jax.random.fold_in(key, 0)
    base = jnp.clip(jax.random.normal(first, (TOKENS, D), jnp.float32), -5.0, 5.0)
    values = base
    return values.astype(jnp.bfloat16)


def draw_block_bucket(key, part):
    base = jax.random.fold_in(key, 11)
    first, second, third, fourth, fifth = jax.random.split(base, 5)
    picked = min(BLK_DEV, N_SEQ)
    hot_count = max(1, picked // 4)
    hot = (jax.random.permutation(first, N_SEQ) < hot_count).astype(jnp.int32)
    noise = jax.random.randint(second, (N_SEQ, N_SEQ), 0, 1 << 16)
    score = (noise + hot[None, :] * (1 << 17)) * N_SEQ + jnp.arange(N_SEQ, dtype=jnp.int32)[None, :]
    order = jnp.argsort(-score, axis=1).astype(jnp.int32)
    chosen = order[:, :picked]
    shuffle_keys = jax.random.randint(third, (N_SEQ, BLK_DEV), 0, 1 << 16) * BLK_DEV + jnp.arange(BLK_DEV, dtype=jnp.int32)[None, :]
    shuffled = jnp.argsort(shuffle_keys, axis=1).astype(jnp.int32)
    owner = jnp.take_along_axis(chosen, shuffled % picked, axis=1).reshape(NBLK)
    random_order = jax.random.randint(fourth, (NBLK,), 0, 1 << 16) * NBLK + jnp.arange(NBLK, dtype=jnp.int32)
    before = (owner[:, None] == owner[None, :]) & (random_order[None, :] < random_order[:, None])
    rank = jnp.sum(before.astype(jnp.int32), axis=1)
    shift = jax.random.randint(fifth, (N_SEQ,), 0, BMAX)
    local = (rank + jnp.take(shift, owner)) // BMAX
    return (owner * BUCK_OWN + local).astype(jnp.int32)


def shard_levels(own_key, extent, cuts, smallest, largest):
    gain = 1.0
    for dim, parts in cuts:
        draws = jax.random.uniform(jax.random.fold_in(jax.random.fold_in(own_key, 6), dim), (parts,), jnp.float32, smallest / len(cuts), largest / len(cuts))
        gain = gain * jnp.repeat(jnp.exp(draws), extent[dim] // parts).reshape((-1,) + (1,) * (len(extent) - 1 - dim))
    return gain


def centred(key, dims, spread, limit, pieces=(), kind=jnp.bfloat16):
    gain = shard_levels(key, dims, pieces, -0.22, 0.18) if pieces else 1.0
    entries = jax.random.normal(key, dims, jnp.float32) * spread * gain
    return jnp.minimum(jnp.maximum(entries, -limit), limit).astype(kind)


def setup_inputs(seed: int = 0) -> dict:
    key_of = jax.random.split(jax.random.key(seed), 7)
    return {
        "tokens": draw_tokens(jax.random.fold_in(key_of[6], 71), 0),
        "w_query": centred(key_of[1], (D, HEADS * HDIM), D ** -0.5, 0.09375, ((1, 4),)),
        "w_key": centred(key_of[2], (D, HEADS * HDIM), D ** -0.5, 0.09375, ((1, 4),)),
        "w_value": centred(key_of[3], (D, HEADS * HDIM), D ** -0.5, 0.09375, ((1, 4),)),
        "w_out": centred(key_of[4], (HEADS * HDIM, D), (HEADS * HDIM) ** -0.5, 0.125, ((0, 4),)),
        "block_bucket": draw_block_bucket(jax.random.fold_in(key_of[6], 71), 0),
    }


def key_lists(bucket, valid):
    count = bucket.shape[0]
    match = (bucket[:, None] == bucket[None, :]) & valid[None, :]
    rank = jnp.cumsum(match.astype(jnp.int32), axis=1) - 1
    picks = match[:, :, None] & (rank[:, :, None] == jnp.arange(BMAX, dtype=jnp.int32)[None, None, :])
    places = jnp.arange(count, dtype=jnp.int32)[None, :, None]
    index = jnp.sum(jnp.where(picks, places, 0), axis=1).astype(jnp.int32)
    usable = jnp.any(picks, axis=1)
    return index, usable


def attend(query, keys, values, usable):
    scores = jnp.einsum("qhd,khd->hqk", query.astype(jnp.float32), keys.astype(jnp.float32)) * (HDIM ** -0.5)
    scores = jnp.where(usable[None, None, :], scores, -1e30)
    top = jnp.max(scores, axis=-1, keepdims=True)
    expo = jnp.exp(scores - top)
    weights = (expo / jnp.sum(expo, axis=-1, keepdims=True)).astype(jnp.bfloat16)
    mixed = jnp.einsum("hqk,khd->qhd", weights.astype(jnp.float32), values.astype(jnp.float32))
    return mixed.astype(jnp.bfloat16)


def reference(tokens, w_query, w_key, w_value, w_out, block_bucket):
    query = jnp.dot(tokens, w_query, preferred_element_type=jnp.float32).astype(jnp.bfloat16)
    keys = jnp.dot(tokens, w_key, preferred_element_type=jnp.float32).astype(jnp.bfloat16)
    values = jnp.dot(tokens, w_value, preferred_element_type=jnp.float32).astype(jnp.bfloat16)
    query = query.reshape(NBLK, BLOCK, HEADS, HDIM)
    keys = keys.reshape(NBLK, BLOCK, HEADS, HDIM)
    values = values.reshape(NBLK, BLOCK, HEADS, HDIM)
    index, usable = key_lists(block_bucket, jnp.ones((NBLK,), dtype=bool))

    def one_block(which):
        picked = index[which]
        key_rows = jnp.take(keys, picked, axis=0).reshape(BMAX * BLOCK, HEADS, HDIM)
        value_rows = jnp.take(values, picked, axis=0).reshape(BMAX * BLOCK, HEADS, HDIM)
        mask = jnp.repeat(usable[which], BLOCK)
        return attend(query[which], key_rows, value_rows, mask)

    mixed = lax.map(one_block, jnp.arange(NBLK, dtype=jnp.int32))
    mixed = mixed.reshape(TOKENS, HEADS * HDIM)
    return jnp.dot(mixed, w_out, preferred_element_type=jnp.float32).astype(jnp.bfloat16)
```

```python
import functools

import jax
import jax.numpy as jnp
from jax import lax
from jax.experimental import pallas as pl
from jax.experimental.pallas import tpu as pltpu
from jax.sharding import PartitionSpec as P

HDIM = 128
CHUNKS = 2
F32 = jnp.float32
BF16 = jnp.bfloat16
I32 = jnp.int32


def swap(x, axis, mask):
    size = lax.axis_size(axis)
    return lax.ppermute(x, axis, [(i, i ^ mask) for i in range(size)])


def mm(a, b):
    return jnp.dot(a, b, preferred_element_type=F32)


def call(kernel, grid, prefetch, in_specs, out_specs, out_shape, scratch=(), aliases=None):
    return pl.pallas_call(
        kernel,
        grid_spec=pltpu.PrefetchScalarGridSpec(
            num_scalar_prefetch=prefetch,
            grid=grid,
            in_specs=in_specs,
            out_specs=out_specs,
            scratch_shapes=list(scratch),
        ),
        out_shape=out_shape,
        input_output_aliases=aliases or {},
    )


def full(shape):
    return pl.BlockSpec(shape, lambda *_: (0,) * len(shape))


def early_kernel(pos, own, near, w_key, w_value, out):
    step = pl.program_id(0)
    width = w_key.shape[1]

    @pl.when(step == 0)
    def _():
        out[:, :width] = mm(own[...], w_key[...])
        out[:, width:] = mm(own[...], w_value[...])

    @pl.when(step == 1)
    def _():
        out[:, :width] += mm(near[...], w_key[...])
        out[:, width:] += mm(near[...], w_value[...])


def early(pos, own, near, w_key, w_value):
    rows, part = own.shape
    width = w_key.shape[1]
    weight = pl.BlockSpec((part, width), lambda p, pos: (pos[0] ^ p, 0))
    return call(
        early_kernel,
        (2,),
        1,
        [full(own.shape), full(own.shape), weight, weight],
        full((rows, 2 * width)),
        jax.ShapeDtypeStruct((rows, 2 * width), F32),
    )(pos, own, near, w_key, w_value)


def late_kernel(splits, pos, acc, far, far_near, w_key, w_value, *refs):
    outs, total, kept = refs[:-2], refs[-2], refs[-1]
    step = pl.program_id(0)
    width = w_key.shape[1]
    units, blocks, block_len, _ = kept.shape
    heads = width // HDIM

    @pl.when(step == 0)
    def _():
        total[:, :width] = acc[:, :width] + mm(far[...], w_key[...])
        total[:, width:] = acc[:, width:] + mm(far[...], w_value[...])

    @pl.when(step == 1)
    def _():
        key = (total[:, :width] + mm(far_near[...], w_key[...])).astype(BF16)
        value = (total[:, width:] + mm(far_near[...], w_value[...])).astype(BF16)
        for head in range(heads):
            cols = slice(head * HDIM, (head + 1) * HDIM)
            kept[head] = key[:, cols].reshape(blocks, block_len, HDIM)
            kept[heads + head] = value[:, cols].reshape(blocks, block_len, HDIM)
        rows = block_len // splits
        for m, out in enumerate(outs):
            piece = pos[1] ^ m
            if splits == 1:
                out[...] = kept[piece]
            else:
                first = pl.multiple_of((piece % splits) * rows, rows)
                out[...] = kept[piece // splits, :, pl.ds(first, rows), :]


def late(pos, chunk, block_len, seq_count, acc, far, far_near, w_key, w_value):
    rows, part = far.shape
    width = w_key.shape[1]
    units = 2 * (width // HDIM)
    splits = seq_count // units
    blocks = rows // block_len
    weight = pl.BlockSpec((part, width), lambda p, pos: (pos[0] ^ (p + 2), 0))
    piece = (blocks, block_len // splits, HDIM)
    return call(
        functools.partial(late_kernel, splits),
        (2,),
        1,
        [
            pl.BlockSpec((rows, 2 * width), lambda p, pos: (chunk, 0)),
            full(far.shape),
            full(far.shape),
            weight,
            weight,
        ],
        [full(piece)] * seq_count,
        [jax.ShapeDtypeStruct(piece, BF16)] * seq_count,
        [pltpu.VMEM((rows, 2 * width), F32), pltpu.VMEM((units, blocks, block_len, HDIM), BF16)],
    )(pos, acc, far, far_near, w_key, w_value)


def query_kernel(chunks, pos, own, near, *refs):
    far, far_near = refs[:chunks], refs[chunks : 2 * chunks]
    w_query, out, total = refs[2 * chunks :]
    step = pl.program_id(0)
    rows = own.shape[0] // chunks

    @pl.when(step == 0)
    def _():
        total[...] = mm(own[...], w_query[...])

    @pl.when(step == 1)
    def _():
        total[...] += mm(near[...], w_query[...])

    @pl.when(step == 2)
    def _():
        for c in range(chunks):
            span = slice(c * rows, (c + 1) * rows)
            total[span] += mm(far[c][...], w_query[...])

    @pl.when(step == 3)
    def _():
        for c in range(chunks):
            span = slice(c * rows, (c + 1) * rows)
            out[span] = (total[span] + mm(far_near[c][...], w_query[...])).astype(BF16)


def queries(pos, own, near, far, far_near, w_query):
    rows, part = own.shape
    width = w_query.shape[1]
    chunks = len(far)
    return call(
        functools.partial(query_kernel, chunks),
        (4,),
        1,
        [full(own.shape)] * 2
        + [full(far[0].shape)] * (2 * chunks)
        + [pl.BlockSpec((part, width), lambda p, pos: (pos[0] ^ p, 0))],
        full((rows, width)),
        jax.ShapeDtypeStruct((rows, width), BF16),
        [pltpu.VMEM((rows, width), F32)],
    )(pos, own, near, *far, *far_near, w_query)


def choose_kernel(count, seq_count, index, *refs):
    pieces, outs, table = refs[:count], refs[count : 2 * count], refs[-1]
    blocks = pieces[0].shape[0]
    chunks = count // seq_count
    for c in range(chunks):
        for m in range(seq_count):
            first = (m * chunks + c) * blocks
            table[first : first + blocks] = pieces[c * seq_count + m][...]
    for c in range(chunks):
        for m in range(seq_count):
            for i in range(blocks):
                outs[c * seq_count + m][i] = table[index[(m * chunks + c) * blocks + i]]


def choose(index, pieces, seq_count):
    count = len(pieces)
    shape = pieces[0].shape
    return call(
        functools.partial(choose_kernel, count, seq_count),
        (1,),
        1,
        [full(shape)] * count,
        [full(shape)] * count,
        [jax.ShapeDtypeStruct(shape, BF16)] * count,
        [pltpu.VMEM((count * shape[0],) + shape[1:], BF16)],
    )(index, *pieces)


def attend_kernel(splits, chunk, pos, paired, query, *refs):
    count = (len(refs) - 3) // 2
    own_parts, other_parts = refs[:count], refs[count : 2 * count]
    out, own, other = refs[2 * count :]
    units, blocks, block_len, _ = own.shape
    heads = units // 2
    rows = block_len // splits
    for m in range(count):
        piece = pos[1] ^ m
        if splits == 1:
            own[piece] = own_parts[m][...]
            other[piece] = other_parts[m][...]
        else:
            first = pl.multiple_of((piece % splits) * rows, rows)
            own[piece // splits, :, pl.ds(first, rows), :] = own_parts[m][...]
            other[piece // splits, :, pl.ds(first, rows), :] = other_parts[m][...]
    dims = (((1,), (1,)), ((), ()))
    for b in range(blocks):
        has = paired[chunk * blocks + b] > 0
        for h in range(heads):
            q = query[b * block_len : (b + 1) * block_len, h * HDIM : (h + 1) * HDIM]
            here = lax.dot_general(q, own[h, b], dims, preferred_element_type=F32)
            there = lax.dot_general(q, other[h, b], dims, preferred_element_type=F32)
            here = here * HDIM ** (-0.5)
            there = jnp.where(has, there * HDIM ** (-0.5), -1e30)
            top = jnp.maximum(
                jnp.max(here, axis=-1, keepdims=True), jnp.max(there, axis=-1, keepdims=True)
            )
            here = jnp.exp(here - top)
            there = jnp.exp(there - top)
            norm = jnp.sum(here, axis=-1, keepdims=True) + jnp.sum(there, axis=-1, keepdims=True)
            mixed = mm((here / norm).astype(BF16), own[heads + h, b])
            mixed += mm((there / norm).astype(BF16), other[heads + h, b])
            out[b * block_len : (b + 1) * block_len, h * HDIM : (h + 1) * HDIM] = mixed.astype(BF16)


def attend(pos, paired, chunk, block_len, query, own_parts, other_parts):
    count = len(own_parts)
    shape = own_parts[0].shape
    splits = block_len // shape[1]
    rows = shape[0] * block_len
    width = query.shape[1]
    kept = pltpu.VMEM((count // splits, shape[0], block_len, HDIM), BF16)
    return call(
        functools.partial(attend_kernel, splits, chunk),
        (1,),
        2,
        [pl.BlockSpec((rows, width), lambda *_: (chunk, 0))] + [full(shape)] * (2 * count),
        full((rows, width)),
        jax.ShapeDtypeStruct((rows, width), BF16),
        [kept, kept],
    )(pos, paired, query, *own_parts, *other_parts)


def project_kernel(pos, *refs):
    parts, weights, out = refs[:4], refs[4:8], refs[-1]
    total = mm(parts[0][...], weights[0][...])
    for part, weight in zip(parts[1:], weights[1:]):
        total += mm(part[...], weight[...])
    out[...] = total.astype(BF16)


def project(pos, chunk, chunks, parts, w_out, weights, before):
    rows, width = parts[0].shape
    columns = weights[0].shape[1]
    spec = pl.BlockSpec((rows, columns), lambda *_: (chunk, 0))
    in_specs = (
        [full((rows, width))] * 4
        + [pl.BlockSpec((width, columns), lambda _, pos: (0, pos[0]))]
        + [full((width, columns))] * 3
    )
    args = [pos, *parts, w_out, *weights]
    aliases = None
    if before is not None:
        in_specs.append(pl.BlockSpec(memory_space=pl.ANY))
        args.append(before)
        aliases = {len(args) - 1: 0}
    return call(
        project_kernel,
        (1,),
        1,
        in_specs,
        spec,
        jax.ShapeDtypeStruct((rows * chunks, columns), BF16),
        aliases=aliases,
    )(*args)


def out_weights(w_out, gate, seq, head, columns):
    half = w_out.shape[0] // 2
    side = seq % 2
    w_out, _ = lax.optimization_barrier((w_out, gate))
    near = swap(lax.dynamic_slice_in_dim(w_out, (head ^ 1) * columns, columns, 1), "head", 1)
    found = [near]
    for mask in (2, 3):
        cut = lax.dynamic_slice(w_out, (side * half, (head ^ mask) * columns), (half, columns))
        mine = swap(cut, "head", mask)
        theirs = swap(mine, "seq", 1)
        upper = jnp.where(side == 0, mine, theirs)
        lower = jnp.where(side == 0, theirs, mine)
        found.append(jnp.concatenate([upper, lower], axis=0))
    return found


def per_device(tokens, w_query, w_key, w_value, w_out, block_bucket):
    seq_count = lax.axis_size("seq")
    seq = lax.axis_index("seq").astype(I32)
    head = lax.axis_index("head").astype(I32)
    blocks = block_bucket.shape[0]
    tok_here = tokens.shape[0]
    block_len = tok_here // blocks
    columns = w_out.shape[1] // lax.axis_size("head")
    chunks = CHUNKS
    rows = tok_here // chunks
    pos = jnp.stack([head, seq])

    ids = block_bucket
    mask = 1
    while mask < seq_count:
        ids = jnp.concatenate([ids, swap(ids, "seq", mask)])
        mask *= 2
    place = jnp.arange(ids.shape[0], dtype=I32)
    match = (ids[:, None] == ids[None, :]) & (place[:, None] != place[None, :])
    index = jnp.sum(jnp.where(match, place[None, :], 0), axis=1).astype(I32)
    paired = jnp.any(match, axis=1).astype(I32)[:blocks]

    near = swap(tokens, "head", 1)
    far = [swap(tokens[c * rows : (c + 1) * rows], "head", 2) for c in range(chunks)]
    far_near = [swap(part, "head", 1) for part in far]
    acc = early(pos, tokens, near, w_key, w_value)

    own_parts, first_hop = [], []
    for c in range(chunks):
        parts = late(pos, c, block_len, seq_count, acc, far[c], far_near[c], w_key, w_value)
        own_parts.append(parts)
        first_hop += [parts[0]] + [swap(parts[m], "seq", m) for m in range(1, seq_count)]
    query = queries(pos, tokens, near, far, far_near, w_query)
    weights = out_weights(w_out, far[-1], seq, head, columns)

    chosen = choose(index, first_hop, seq_count)
    out = None
    for c in range(chunks):
        parts = chosen[c * seq_count : (c + 1) * seq_count]
        parts = [parts[0]] + [swap(parts[m], "seq", m) for m in range(1, seq_count)]
        mixed = attend(pos, paired, c, block_len, query, own_parts[c], parts)
        mixed_near = swap(mixed, "head", 1)
        mixed_far = swap(mixed, "head", 2)
        mixed_far_near = swap(mixed_far, "head", 1)
        group = [mixed, mixed_near, mixed_far, mixed_far_near]
        out = project(pos, c, chunks, group, w_out, weights, out)
    return out


def solution(mesh):
    placed = (
        P("seq", "head"),
        P(None, "head"),
        P(None, "head"),
        P(None, "head"),
        P("head", None),
        P("seq"),
    )
    return jax.shard_map(
        per_device, mesh=mesh, in_specs=placed, out_specs=P("seq", "head"), check_vma=False
    )
```
